256 devices in a mesh: seg: 4 (over y_hi, core), mic: 64 (over z, x, y_lo).
Axes of the slice: x: 4, y: 4 (y_hi: 2, y_lo: 2; y = y_hi * 2 + y_lo), z: 8, core: 2. Of those that a mesh axis runs over, the one named last changes fastest.
Arguments:
- time_data: bfloat16 [128, 4096, 1024], P('seg', 'mic'), may hold values from -6 to 6
- order_bin: int32 [1], replicated, may hold values from 32 to 203
- mic_pos: int32 [3, 4096], replicated, may hold values from -2000 to 2000
- grid_pos: int32 [3, 131072], P(None, 'mic'), may hold values from -1500 to 1500
Outputs:
- beam_power: float32 [64, 2048], P('mic', 'seg')
The draws below stay inside these ranges and needn't reach their ends.
All inputs are finite; a program needn't handle non-finite values.
Results may differ from the reference program's by a relative error of at most 0.00083.
Values may be sent and summed in bfloat16 or wider, within the bound.
A program may use at most 256 MiB of HBM per device.

```python
import math
import jax
import jax.numpy as jnp
from jax import lax

L = 1024
MIC = 4096
SEG = 128
SLAB = 2048
GRID = 131072
N_MIC = 64


def place_ends(array, key, smallest, largest):
    longest = array.shape.index(max(array.shape))
    spots = []
    for shift in (0, 1):
        where = [jax.random.randint(jax.random.fold_in(key, axis), (), 0, length) for axis, length in enumerate(array.shape)]
        where[longest] = (where[longest] + shift) % array.shape[longest]
        spots.append(tuple(where))
    return array.at[spots[0]].set(smallest).at[spots[1]].set(largest)


def levels(own_key, dims, shards, low, high):
    level = 1.0
    for axis_at, parts in shards:
        steps = jax.random.uniform(jax.random.fold_in(jax.random.fold_in(own_key, 6), axis_at), (parts,), jnp.float32, low / len(shards), high / len(shards))
        level = level * jnp.repeat(jnp.exp(steps), dims[axis_at] // parts).reshape((-1,) + (1,) * (len(dims) - 1 - axis_at))
    return level


def normal_values(rng, shape, deviation, reach, cuts=(), held_as=jnp.bfloat16):
    drawn = deviation * jax.random.normal(rng, shape, jnp.float32)
    if cuts:
        drawn = drawn * levels(rng, shape, cuts, -0.22, 0.18)
    return jnp.clip(drawn, -reach, reach).astype(held_as)


def setup_inputs(seed: int = 0) -> dict:
    key_list = jax.random.split(jax.random.key(seed), 5)
    return {
        "time_data": normal_values(key_list[0], (SEG, MIC, L), 1.0, 6.0, ((0, 4), (1, 64))),
        "order_bin": jax.random.randint(key_list[1], (1,), L // 32, L // 5).astype(jnp.int32),
        "mic_pos": place_ends(jax.random.randint(key_list[2], (3, MIC), -2000, 2001), jax.random.fold_in(key_list[2], 1), -2000, 2000).astype(jnp.int32),
        "grid_pos": place_ends(jax.random.randint(key_list[3], (3, GRID), -1500, 1501), jax.random.fold_in(key_list[3], 1), -1500, 1500).astype(jnp.int32),
    }


def spectral_table(order_value, samples):
    times = jnp.arange(samples, dtype=jnp.int32)
    turned = order_value * times % samples
    angle = turned.astype(jnp.float32) * (2.0 * math.pi / samples)
    window = 0.5 - 0.5 * jnp.cos(times.astype(jnp.float32) * (2.0 * math.pi / samples))
    return jnp.stack([window * jnp.cos(angle), -(window * jnp.sin(angle))]).astype(jnp.bfloat16)

def stacked_left(spectra):
    real_part = spectra[0]
    imag_part = spectra[1]
    upper = jnp.concatenate([real_part, -imag_part], axis=1)
    lower = jnp.concatenate([imag_part, real_part], axis=1)
    return jnp.concatenate([upper, lower], axis=0)

def beam_block(left, mic_part, points, wave):
    offsets = (points[:, None, :] - mic_part[:, :, None]).astype(jnp.float32) * 0.001
    distance = jnp.sqrt(offsets[0] * offsets[0] + offsets[1] * offsets[1] + offsets[2] * offsets[2])
    phase = wave * distance
    steering = jnp.concatenate([jnp.cos(phase), jnp.sin(phase)], axis=0).astype(jnp.bfloat16)
    return jnp.dot(left, steering, preferred_element_type=jnp.float32)

def reference(time_data, order_bin, mic_pos, grid_pos):
    table = spectral_table(order_bin[0], L)
    rows = time_data.reshape(SEG * MIC, L)
    spec = jnp.dot(rows, table.T, preferred_element_type=jnp.float32)
    spectra = spec.T.reshape(2, SEG, MIC).astype(jnp.bfloat16)
    wave = order_bin[0].astype(jnp.float32) * jnp.float32(2.0 * math.pi * 51200.0 / 343.0) / jnp.float32(L)
    left = stacked_left(spectra)
    denom = jnp.float32(SEG * MIC * 0.375 * L)
    block = math.gcd(GRID, 512)
    blocks = grid_pos.reshape(3, GRID // block, block).transpose(1, 0, 2)

    def one_block(points):
        beams = beam_block(left, mic_pos, points, wave)
        return lax.optimization_barrier(jnp.sum(beams * beams, axis=0)) / denom
    return lax.map(one_block, blocks).reshape(N_MIC, SLAB)
```

```python
import functools
import math

import jax
import jax.numpy as jnp
from jax import lax
from jax.experimental import pallas as pl
from jax.experimental.pallas import tpu as pltpu
from jax.sharding import PartitionSpec as P

MESH = pl.DeviceIdType.MESH
F32 = jnp.float32
BF16 = jnp.bfloat16

NX, NY, NZ = 4, 4, 8
SIN = (4.442882834149665, -7.308241154529405, 3.6062889579421076, -0.8457635944249917, 0.10920575020378133)
COS = (1.414213496564824, -6.978850988209009, 5.739461169968767, -1.8835629820109427, 0.3106981797730274)
SIN_SHORT = (4.442867902991959, -7.3074434197428175, 3.5947880638880885, -0.7843739922969518)
COS_SHORT = (1.4142040804388327, -6.977642054046934, 5.715238359077324, -1.728348549561637)


def horner(coefs, z):
    total = jnp.full_like(z, coefs[-1])
    for c in coefs[-2::-1]:
        total = total * z + c
    return total


def cos_sin_turns(turns, sin_coefs, cos_coefs):
    r = turns - jnp.round(turns)
    z = r * r
    s = r * horner(sin_coefs, z)
    c = horner(cos_coefs, z)
    return 1.0 - s * s, s * c


def device(y, z, x, core):
    return {"seg": (y // 2) * 2 + core, "mic": (z * NX + x) * 2 + y % 2}


def kernel(
    time_ref, bin_ref, mic_ref, grid_ref, out_ref,
    tbuf, wt, own, inbox, gathered, cosb, sinb, accp, accq, micf, pointf,
    t_sem, p_send, p_recv, z_send, z_recv, m_send, m_recv, l_send, l_recv, f_send, f_recv,
):
    seg = lax.axis_index("seg")
    mic = lax.axis_index("mic")
    core = seg % 2
    y_hi, y_lo = seg // 2, mic % 2
    y = y_hi * 2 + y_lo
    x = (mic // 2) % NX
    z = mic // (2 * NX)
    sibling = device(y, z, x, 1 - core)
    z_peer = [device(y, (z + d) % NZ, x, core) for d in range(NZ)]
    x_peer = [device(y, z, (x + d) % NX, core) for d in range(NX)]
    y_peer = [device((y + d) % NY, z, x, core) for d in range(NY)]

    barrier = pltpu.get_barrier_semaphore()
    peers = [sibling] + z_peer[1:] + x_peer[1:] + y_peer[1:]
    for peer in peers:
        pl.semaphore_signal(barrier, inc=1, device_id=peer, device_id_type=MESH)

    seg_dev, mic_dev, samples = time_ref.shape
    chunks = tbuf.shape[0]
    per = seg_dev // chunks

    def time_copy(i):
        return pltpu.make_async_copy(time_ref.at[pl.ds(i * per, per)], tbuf.at[i], t_sem.at[i])

    for i in range(chunks):
        time_copy(i).start()

    order = bin_ref[0]
    t = lax.broadcasted_iota(jnp.int32, (8, samples), 1)
    turned = (order * t) & (samples - 1)
    inv = 1.0 / samples
    wcos, _ = cos_sin_turns(t.astype(F32) * inv, SIN, COS)
    ca, sa = cos_sin_turns(turned.astype(F32) * inv, SIN, COS)
    window = 0.5 - 0.5 * wcos
    row_re = (window * ca).astype(BF16).astype(F32)
    row_im = (-(window * sa)).astype(BF16).astype(F32)
    wt[...] = jnp.concatenate([row_re] * 8 + [row_im] * 8, axis=0).astype(BF16)

    def split(v):
        coarse = jnp.floor(v * (1.0 / 64.0) + 0.5) * 64.0
        return coarse, v - coarse

    def split3(v):
        top = jnp.floor(v * (1.0 / 65536.0)) * 65536.0
        rest = v - top
        mid = jnp.floor(rest * (1.0 / 256.0)) * 256.0
        return top, mid, rest - mid

    width = out_ref.shape[1]
    pts = grid_ref[:, pl.ds(pl.multiple_of(seg * width, 128), width)].astype(F32)
    mics = mic_ref[...].astype(F32)

    def rows_of(v, fold):
        hi, lo = split(v)
        sq = v * v
        top, mid, low = split3(sq[0:1] + sq[1:2] + sq[2:3])
        one = jnp.ones_like(top)
        tiny = jnp.full_like(top, 2.0**-20)
        zero = jnp.zeros((13, v.shape[1]), F32)
        if fold:
            return jnp.concatenate([-2.0 * hi, -2.0 * hi, -2.0 * lo, -2.0 * lo, one, one, one, top, mid, low, tiny, zero], axis=0)
        return jnp.concatenate([hi, lo, hi, lo, top, mid, low, one, one, one, tiny, zero], axis=0)

    micf[...] = rows_of(mics, True).astype(BF16)
    pointf[...] = rows_of(pts, False).T.astype(BF16)
    turns_per_mm = order.astype(F32) * F32(0.001 * 51200.0 / 343.0 / samples)

    lane = lax.broadcasted_iota(jnp.int32, (mic_dev, 128), 1) & 63

    def spectrum(i, acc):
        time_copy(i).wait()
        part = lax.dot_general(
            tbuf[i].reshape(per * mic_dev, samples), wt[...], (((1,), (1,)), ((), ())),
            preferred_element_type=F32,
        )
        for k in range(per):
            hit = lane == core * seg_dev + i * per + k
            acc = jnp.where(hit, part[k * mic_dev:(k + 1) * mic_dev], acc)
        return acc

    acc = lax.fori_loop(0, chunks, spectrum, jnp.zeros((mic_dev, 128), F32))
    own[...] = acc.astype(BF16).reshape(4, 16, 128)

    half = pl.ds(2 * core, 2)
    pl.semaphore_wait(barrier, len(peers))

    def push(src, dst, send, recv, peer):
        return pltpu.make_async_remote_copy(
            src_ref=src, dst_ref=dst, send_sem=send, recv_sem=recv, device_id=peer, device_id_type=MESH
        )

    pair = push(own.at[pl.ds(2 * (1 - core), 2)], inbox, p_send, p_recv, sibling)
    pair.start()

    blocks = cosb.shape[2] // 256
    tall = 128

    def steer(j, carry):
        g = j // blocks
        at = pl.ds(pl.multiple_of((j % blocks) * 256, 256), 256)
        feat = micf[:, pl.ds(pl.multiple_of(j * 256, 256), 256)]
        for i in range(width // tall):
            rows = pl.ds(i * tall, tall)
            d2 = jnp.dot(pointf[rows, :], feat, preferred_element_type=F32)
            turns = (d2 * turns_per_mm) * lax.rsqrt(d2)
            ca, sa = cos_sin_turns(turns, SIN_SHORT, COS_SHORT)
            cosb[g, rows, at] = ca.astype(BF16)
            sinb[g, rows, at] = sa.astype(BF16)
        return carry

    lax.fori_loop(0, 2, steer, 0)
    pair.wait()
    mine = gathered.at[y_hi, z, x, y_lo, half]
    mine[...] = own[half] + inbox[...]

    z_out = []
    for d in range(1, NZ):
        c = push(mine, mine, z_send.at[d], z_recv.at[d], z_peer[d])
        c.start()
        z_out.append(c)
    lax.fori_loop(2, 5, steer, 0)
    for d in range(1, NZ):
        src = gathered.at[y_hi, (z + NZ - d) % NZ, x, y_lo, half]
        push(src, src, z_send.at[d], z_recv.at[d], z_peer[d]).wait_recv()

    q1, q2 = 2 * core, 2 * core + 1
    m_out = []
    for d in range(1, NX):
        line = gathered.at[y_hi, :, x, y_lo, q1]
        c = push(line, line, m_send.at[0, d], m_recv.at[0, d], x_peer[d])
        c.start()
        m_out.append(c)
    for d in range(1, NY):
        line = gathered.at[y_hi, :, x, y_lo, q2]
        c = push(line, line, m_send.at[1, d], m_recv.at[1, d], y_peer[d])
        c.start()
        m_out.append(c)
    lax.fori_loop(5, 8, steer, 0)
    for d in range(1, NX):
        line = gathered.at[y_hi, :, (x + NX - d) % NX, y_lo, q1]
        push(line, line, m_send.at[0, d], m_recv.at[0, d], x_peer[d]).wait_recv()
    for d in range(1, NY):
        yy = (y + NY - d) % NY
        line = gathered.at[yy // 2, :, x, yy % 2, q2]
        push(line, line, m_send.at[1, d], m_recv.at[1, d], y_peer[d]).wait_recv()

    def plane1(yy):
        return gathered.at[yy // 2, :, :, yy % 2, q1]

    def plane2(xx):
        return gathered.at[:, :, xx, :, q2]

    def plane1_in(yy):
        return gathered.at[yy // 2, :, :, yy % 2, 2 * (1 - core)]

    def plane2_in(xx):
        return gathered.at[:, :, xx, :, 2 * (1 - core) + 1]

    l_out = []
    for d in range(1, NY):
        c = push(plane1(y), plane1(y), l_send.at[0, d], l_recv.at[0, d], y_peer[d])
        c.start()
        l_out.append(c)
        c = push(plane2(x), plane2(x), l_send.at[1, d], l_recv.at[1, d], x_peer[d])
        c.start()
        l_out.append(c)
    f_out = []

    def forward(d):
        yy, xx = (y + NY - d) % NY, (x + NX - d) % NX
        for k, p in ((0, plane1(yy)), (1, plane2(xx))):
            c = push(p, p, f_send.at[k, d], f_recv.at[k, d], sibling)
            c.start()
            f_out.append(c)

    forward(0)
    lax.fori_loop(8, 16, steer, 0)
    for d in (1, 3, 2):
        yy, xx = (y + NY - d) % NY, (x + NX - d) % NX
        push(plane1(yy), plane1(yy), l_send.at[0, d], l_recv.at[0, d], y_peer[d]).wait_recv()
        push(plane2(xx), plane2(xx), l_send.at[1, d], l_recv.at[1, d], x_peer[d]).wait_recv()
        forward(d)
    for d in range(NY):
        yy, xx = (y + NY - d) % NY, (x + NX - d) % NX
        p = plane1_in(yy)
        push(p, p, f_send.at[0, d], f_recv.at[0, d], sibling).wait_recv()
        p = plane2_in(xx)
        push(p, p, f_send.at[1, d], f_recv.at[1, d], sibling).wait_recv()

    accp[...] = jnp.zeros_like(accp)
    accq[...] = jnp.zeros_like(accq)
    groups = cosb.shape[0]
    zs = NZ // groups

    def beams(g, carry):
        left = gathered[0, pl.ds(g * zs, zs)].reshape(cosb.shape[2], 128)
        right = gathered[1, pl.ds(g * zs, zs)].reshape(cosb.shape[2], 128)
        spectra = jnp.concatenate([left, right], axis=1)
        accp[...] += jnp.dot(cosb[g], spectra, preferred_element_type=F32)
        accq[...] += jnp.dot(sinb[g], spectra, preferred_element_type=F32)
        return carry

    lax.fori_loop(0, groups, beams, 0)

    sign = jnp.where(lax.broadcasted_iota(jnp.int32, (width, 128), 1) < 64, -1.0, 1.0)
    power = jnp.zeros((width, 128), F32)
    for k in range(2):
        cols = pl.ds(k * 128, 128)
        b = accp[:, cols] + sign * pltpu.roll(accq[:, cols], 64, 1)
        power = power + b * b
    scale = 1.0 / (seg_dev * lax.axis_size("seg") * mic_dev * lax.axis_size("mic") * 0.375 * samples)
    out_ref[...] = jnp.sum(power.T, axis=0, keepdims=True) * scale

    pair_done = []
    for c in z_out + m_out + l_out + f_out + pair_done:
        c.wait_send()


def shards(time_data, order_bin, mic_pos, grid_pos):
    seg_dev, mic_dev, samples = time_data.shape
    width = grid_pos.shape[1] // lax.axis_size("seg")
    mics = mic_pos.shape[1]
    chunks = 8
    dma = pltpu.SemaphoreType.DMA
    return pl.pallas_call(
        kernel,
        out_shape=jax.ShapeDtypeStruct((1, width), F32),
        in_specs=[
            pl.BlockSpec(memory_space=pl.ANY),
            pl.BlockSpec(memory_space=pltpu.SMEM),
            pl.BlockSpec(memory_space=pltpu.VMEM),
            pl.BlockSpec(memory_space=pltpu.VMEM),
        ],
        out_specs=pl.BlockSpec(memory_space=pltpu.VMEM),
        scratch_shapes=[
            pltpu.VMEM((chunks, seg_dev // chunks, mic_dev, samples), BF16),
            pltpu.VMEM((128, samples), BF16),
            pltpu.VMEM((4, 16, 128), BF16),
            pltpu.VMEM((2, 16, 128), BF16),
            pltpu.VMEM((2, NZ, NX, 2, 4, 16, 128), BF16),
            pltpu.VMEM((4, width, mics // 4), BF16),
            pltpu.VMEM((4, width, mics // 4), BF16),
            pltpu.VMEM((width, 256), F32),
            pltpu.VMEM((width, 256), F32),
            pltpu.VMEM((32, mics), BF16),
            pltpu.VMEM((width, 32), BF16),
            dma((chunks,)),
            dma, dma,
            dma((NZ,)), dma((NZ,)),
            dma((2, NX)), dma((2, NX)),
            dma((2, NX)), dma((2, NX)),
            dma((2, NX)), dma((2, NX)),
        ],
        compiler_params=pltpu.CompilerParams(
            collective_id=0, has_side_effects=True, vmem_limit_bytes=48 << 20
        ),
        name="beamform",
    )(time_data, order_bin, mic_pos, grid_pos)


def solution(mesh):
    placed = (P("seg", "mic", None), P(), P(), P(None, "mic"))
    return jax.shard_map(
        shards, mesh=mesh, in_specs=placed, out_specs=P("mic", "seg"), check_vma=False
    )
```

```python
import functools
import math

import jax
import jax.numpy as jnp
from jax import lax
from jax.experimental import pallas as pl
from jax.experimental.pallas import tpu as pltpu
from jax.sharding import PartitionSpec as P

MESH = pl.DeviceIdType.MESH
F32 = jnp.float32
BF16 = jnp.bfloat16

NX, NY, NZ = 4, 4, 8
AT_LINES, AT_PLANES, AT_BEAMS = 2, 7, 13
SIN = (4.442882834149665, -7.308241154529405, 3.6062889579421076, -0.8457635944249917, 0.10920575020378133)
COS = (1.414213496564824, -6.978850988209009, 5.739461169968767, -1.8835629820109427, 0.3106981797730274)
SIN_SHORT = (4.442867902991959, -7.3074434197428175, 3.5947880638880885, -0.7843739922969518)
COS_SHORT = (1.4142040804388327, -6.977642054046934, 5.715238359077324, -1.728348549561637)


def horner(coefs, z):
    total = jnp.full_like(z, coefs[-1])
    for c in coefs[-2::-1]:
        total = total * z + c
    return total


def cos_sin_turns(turns, sin_coefs, cos_coefs):
    r = turns - jnp.round(turns)
    z = r * r
    s = r * horner(sin_coefs, z)
    c = horner(cos_coefs, z)
    return 1.0 - s * s, s * c


def device(y, z, x, core):
    return {"seg": (y // 2) * 2 + core, "mic": (z * NX + x) * 2 + y % 2}


def kernel(
    time_ref, bin_ref, mic_hbm, grid_hbm, out_ref,
    mic_ref, grid_ref, s_sem, tbuf, wt, own, kept, inbox, gathered, cosb, sinb, accp, accq, sent, received, micf, pointf,
    t_sem, p_send, p_recv, z_send, z_recv, m_send, m_recv, l_send, l_recv, b_send, b_recv,
):
    seg = lax.axis_index("seg")
    mic = lax.axis_index("mic")
    core = seg % 2
    y_hi, y_lo = seg // 2, mic % 2
    y = y_hi * 2 + y_lo
    x = (mic // 2) % NX
    z = mic // (2 * NX)
    zp = z // 2
    sibling = device(y, z, x, 1 - core)
    z_peer = [device(y, (z + d) % NZ, x, core) for d in range(NZ)]
    x_peer = [device(y, z, (x + d) % NX, core) for d in range(NX)]
    y_peer = [device((y + d) % NY, z, x, core) for d in range(NY)]

    seg_dev, mic_dev, samples = time_ref.shape
    mic_half = mic_dev // 2
    chunks, per = tbuf.shape[0], tbuf.shape[1]

    def time_copy(i):
        side = (1 - core) if i < chunks // 2 else core
        first = (i % (chunks // 2)) * per
        src = time_ref.at[pl.ds(first, per), pl.ds(side * mic_half, mic_half)]
        return pltpu.make_async_copy(src, tbuf.at[i], t_sem.at[i])

    small = [
        pltpu.make_async_copy(src, dst, s_sem.at[i])
        for i, (src, dst) in enumerate(((mic_hbm, mic_ref), (grid_hbm, grid_ref)))
    ]
    for c in small:
        c.start()
    for i in range(chunks):
        time_copy(i).start()

    barrier = pltpu.get_barrier_semaphore()
    peers = [sibling] + z_peer[1:] + x_peer[1:] + y_peer[1:]
    for peer in peers:
        pl.semaphore_signal(barrier, inc=1, device_id=peer, device_id_type=MESH)

    order = bin_ref[0]
    t = lax.broadcasted_iota(jnp.int32, (8, samples), 1)
    turned = (order * t) & (samples - 1)
    inv = 1.0 / samples
    wcos, _ = cos_sin_turns(t.astype(F32) * inv, SIN, COS)
    ca, sa = cos_sin_turns(turned.astype(F32) * inv, SIN, COS)
    window = 0.5 - 0.5 * wcos
    rows = jnp.concatenate([window * ca] * 8 + [-(window * sa)] * 8, axis=0)
    wt[...] = rows.T.astype(BF16)

    lane = lax.broadcasted_iota(jnp.int32, (mic_half, 128), 1) & 63

    def spectra(first_chunk):
        acc = jnp.zeros((mic_half, 128), F32)
        for i in range(chunks // 2):
            time_copy(first_chunk + i).wait()
            part = jnp.dot(
                tbuf[first_chunk + i].reshape(per * mic_half, samples), wt[...], preferred_element_type=F32
            )
            for k in range(per):
                hit = lane == core * seg_dev + i * per + k
                acc = jnp.where(hit, part[k * mic_half:(k + 1) * mic_half], acc)
        return acc.astype(BF16).reshape(2, 16, 128)

    def push(src, dst, send, recv, peer):
        return pltpu.make_async_remote_copy(
            src_ref=src, dst_ref=dst, send_sem=send, recv_sem=recv, device_id=peer, device_id_type=MESH
        )

    own[...] = spectra(0)
    kept[...] = spectra(chunks // 2)
    pair_copy = push(own, inbox, p_send, p_recv, sibling)
    pl.semaphore_wait(barrier, len(peers))
    pair_copy.start()
    accp[...] = jnp.zeros_like(accp)
    accq[...] = jnp.zeros_like(accq)

    def split(v):
        coarse = jnp.floor(v * (1.0 / 64.0) + 0.5) * 64.0
        return coarse, v - coarse

    def split3(v):
        top = jnp.floor(v * (1.0 / 65536.0)) * 65536.0
        rest = v - top
        mid = jnp.floor(rest * (1.0 / 256.0)) * 256.0
        return top, mid, rest - mid

    def rows_of(v, fold):
        hi, lo = split(v)
        sq = v * v
        top, mid, low = split3(sq[0:1] + sq[1:2] + sq[2:3])
        one = jnp.ones_like(top)
        tiny = jnp.full_like(top, 2.0**-20)
        zero = jnp.zeros((13, v.shape[1]), F32)
        if fold:
            return jnp.concatenate([-2.0 * hi, -2.0 * hi, -2.0 * lo, -2.0 * lo, one, one, one, top, mid, low, tiny, zero], axis=0)
        return jnp.concatenate([hi, lo, hi, lo, top, mid, low, one, one, one, tiny, zero], axis=0)

    for c in small:
        c.wait()
    width = out_ref.shape[1]
    pts = grid_ref[:, pl.ds(pl.multiple_of(y_hi * 2 * width, 128), 2 * width)].astype(F32)
    pointf[...] = rows_of(pts, False).T.astype(BF16)
    mine = gathered.at[y_hi, z, x, y_lo]

    def z_copy(d):
        return push(mine, mine, z_send.at[d], z_recv.at[z], z_peer[d])

    pair_copy.wait_recv()
    mine[...] = kept[...] + inbox[...]
    for d in (4, 3, 5, 2, 6, 1, 7):
        z_copy(d).start()

    every = rows_of(mic_ref[...].astype(F32), True).astype(BF16)
    part = 8 * mic_dev
    parts = every.shape[1] // part
    stacked = jnp.concatenate([every[:, i * part:(i + 1) * part] for i in range(parts)], axis=0)
    src = lax.broadcasted_iota(jnp.int32, (part, part // 2), 0)
    dst = lax.broadcasted_iota(jnp.int32, (part, part // 2), 1)
    wanted = (dst // mic_half) * mic_dev + core * mic_half + (dst & (mic_half - 1))
    pick = jnp.where(src == wanted, 1.0, 0.0).astype(BF16)
    picked = jnp.dot(stacked, pick, preferred_element_type=F32).astype(BF16)
    micf[...] = jnp.concatenate([picked[i * 32:(i + 1) * 32] for i in range(parts)], axis=1)
    turns_per_mm = order.astype(F32) * F32(0.001 * 51200.0 / 343.0 / samples)

    groups, depth = cosb.shape[0], cosb.shape[2]
    blocks = 4
    tall = 128

    def pair(k):
        return (zp + k * (k + 1) // 2) % groups

    def steer(j):
        g = pair(j // blocks)
        feat = micf[:, pl.ds(pl.multiple_of(g * depth, depth), depth)]
        span = 2 * width // blocks
        for i in range(span // tall):
            rows = pl.ds(pl.multiple_of((j % blocks) * span + i * tall, tall), tall)
            d2 = jnp.dot(pointf[rows, :], feat, preferred_element_type=F32)
            turns = (d2 * turns_per_mm) * lax.rsqrt(d2)
            ca, sa = cos_sin_turns(turns, SIN_SHORT, COS_SHORT)
            cosb[g, rows, :] = ca.astype(BF16)
            sinb[g, rows, :] = sa.astype(BF16)

    q1, q2 = 0, 1

    def line(k, yy, xx, q):
        return gathered.at[yy // 2, pl.ds(2 * pair(k), 2), xx, yy % 2, q]

    def plane1(k, yy):
        return gathered.at[yy // 2, pl.ds(2 * pair(k), 2), :, yy % 2, q1]

    def plane2(k, xx):
        return gathered.at[:, pl.ds(2 * pair(k), 2), xx, :, q2]

    def z_arrived(k):
        for b in range(2):
            zz = 2 * pair(k) + b

            @pl.when(zz != z)
            def _():
                src = gathered.at[y_hi, zz, x, y_lo]
                push(src, src, z_send.at[1], z_recv.at[zz], z_peer[1]).wait_recv()

    def line_copies(k, d, back):
        xx, yy = ((x + NX - d) % NX, (y + NY - d) % NY) if back else (x, y)
        p1, p2 = line(k, y, xx, q1), line(k, yy, x, q2)
        return (
            push(p1, p1, m_send.at[0, k, d], m_recv.at[0, k, d], x_peer[d]),
            push(p2, p2, m_send.at[1, k, d], m_recv.at[1, k, d], y_peer[d]),
        )

    def plane_copies(k, d, back):
        xx, yy = ((x + NX - d) % NX, (y + NY - d) % NY) if back else (x, y)
        p1, p2 = plane1(k, yy), plane2(k, xx)
        return (
            push(p1, p1, l_send.at[0, k, d], l_recv.at[0, k, d], y_peer[d]),
            push(p2, p2, l_send.at[1, k, d], l_recv.at[1, k, d], x_peer[d]),
        )

    def begin(copies, k):
        for d in (2, 1, 3):
            for c in copies(k, d, False):
                c.start()

    def arrived(copies, k):
        for d in (1, 3, 2):
            for c in copies(k, d, True):
                c.wait_recv()

    def flown(copies, k):
        for d in (1, 3, 2):
            for c in copies(k, d, False):
                c.wait_send()

    piece = width // 2

    sign = jnp.where(lax.broadcasted_iota(jnp.int32, (piece, 128), 1) < 64, -1.0, 1.0)

    def rows_at(side, r):
        return pl.ds(pl.multiple_of(side * width + r * piece, piece), piece)

    def beam_copy(r):
        return push(sent.at[r], received.at[r], b_send.at[r], b_recv.at[r], sibling)

    def combined(rows, c):
        cols = pl.ds(c * 128, 128)
        return accp[rows, cols] + sign * pltpu.roll(accq[rows, cols], 64, 1)

    def beams(k, rows):
        g = pair(k)
        zs = pl.ds(2 * g, 2)
        low = gathered[0, zs].reshape(depth, 128)
        high = gathered[1, zs].reshape(depth, 128)
        spec = jnp.concatenate([low, high], axis=1)
        accp[rows, :] += jnp.dot(cosb[g, rows, :], spec, preferred_element_type=F32)
        accq[rows, :] += jnp.dot(sinb[g, rows, :], spec, preferred_element_type=F32)

    steps = groups * blocks

    def step(j, carry):
        pl.when(j < steps)(lambda: steer(j))

        @pl.when((j >= AT_LINES) & (j < AT_LINES + groups))
        def _():
            z_arrived(j - AT_LINES)
            begin(line_copies, j - AT_LINES)

        @pl.when((j >= AT_PLANES) & (j < AT_PLANES + groups))
        def _():
            arrived(line_copies, j - AT_PLANES)
            begin(plane_copies, j - AT_PLANES)

        @pl.when((j >= AT_BEAMS) & (j < AT_BEAMS + groups))
        def _():
            arrived(plane_copies, j - AT_BEAMS)
            def theirs(r, carry):
                rows = rows_at(1 - core, r)
                beams(j - AT_BEAMS, rows)

                @pl.when(j == AT_BEAMS + groups - 1)
                def _():
                    for c in range(2):
                        sent[r, :, pl.ds(c * 128, 128)] = combined(rows, c)
                    beam_copy(r).start()

                return carry

            lax.fori_loop(0, 2, theirs, 0)
            beams(j - AT_BEAMS, pl.ds(pl.multiple_of(core * width, width), width))

        return carry

    lax.fori_loop(0, AT_BEAMS + groups, step, 0)

    scale = 1.0 / (seg_dev * lax.axis_size("seg") * mic_dev * lax.axis_size("mic") * 0.375 * samples)
    for r in range(2):
        mixed = [combined(rows_at(core, r), c) for c in range(2)]
        beam_copy(r).wait_recv()
        power = jnp.zeros((piece, 128), F32)
        for c in range(2):
            b = mixed[c] + received[r, :, pl.ds(c * 128, 128)]
            power = power + b * b
        out_ref[:, pl.ds(r * piece, piece)] = jnp.sum(power.T, axis=0, keepdims=True) * scale

    pair_copy.wait_send()
    for r in range(2):
        beam_copy(r).wait_send()
    for d in range(1, NZ):
        z_copy(d).wait_send()

    def drain(k, carry):
        flown(line_copies, k)
        flown(plane_copies, k)
        return carry

    lax.fori_loop(0, groups, drain, 0)


def shards(time_data, order_bin, mic_pos, grid_pos):
    seg_dev, mic_dev, samples = time_data.shape
    width = grid_pos.shape[1] // lax.axis_size("seg")
    mics = mic_pos.shape[1]
    chunks = 4
    dma = pltpu.SemaphoreType.DMA
    return pl.pallas_call(
        kernel,
        out_shape=jax.ShapeDtypeStruct((1, width), F32),
        in_specs=[
            pl.BlockSpec(memory_space=pltpu.HBM),
            pl.BlockSpec(memory_space=pltpu.SMEM),
            pl.BlockSpec(memory_space=pltpu.HBM),
            pl.BlockSpec(memory_space=pltpu.HBM),
        ],
        out_specs=pl.BlockSpec(memory_space=pltpu.VMEM),
        scratch_shapes=[
            pltpu.VMEM(mic_pos.shape, jnp.int32),
            pltpu.VMEM(grid_pos.shape, jnp.int32),
            pltpu.SemaphoreType.DMA((2,)),
            pltpu.VMEM((chunks, 2 * seg_dev // chunks, mic_dev // 2, samples), BF16),
            pltpu.VMEM((samples, 128), BF16),
            pltpu.VMEM((2, 16, 128), BF16),
            pltpu.VMEM((2, 16, 128), BF16),
            pltpu.VMEM((2, 16, 128), BF16),
            pltpu.VMEM((2, NZ, NX, 2, 2, 16, 128), BF16),
            pltpu.VMEM((4, 2 * width, mics // 8), BF16),
            pltpu.VMEM((4, 2 * width, mics // 8), BF16),
            pltpu.VMEM((2 * width, 256), F32),
            pltpu.VMEM((2 * width, 256), F32),
            pltpu.VMEM((2, width // 2, 256), F32),
            pltpu.VMEM((2, width // 2, 256), F32),
            pltpu.VMEM((32, mics // 2), BF16),
            pltpu.VMEM((2 * width, 32), BF16),
            dma((chunks,)),
            dma, dma,
            dma((NZ,)), dma((NZ,)),
            dma((2, 4, NX)), dma((2, 4, NX)),
            dma((2, 4, NX)), dma((2, 4, NX)),
            dma((2,)), dma((2,)),
        ],
        compiler_params=pltpu.CompilerParams(
            collective_id=0, has_side_effects=True, vmem_limit_bytes=55208 << 10
        ),
        name="beamform",
    )(time_data, order_bin, mic_pos, grid_pos)


def solution(mesh):
    placed = (P("seg", "mic", None), P(), P(), P(None, "mic"))
    return jax.shard_map(
        shards, mesh=mesh, in_specs=placed, out_specs=P("mic", "seg"), check_vma=False
    )
```

```python
import functools
import math

import jax
import jax.numpy as jnp
from jax import lax
from jax.experimental import pallas as pl
from jax.experimental.pallas import tpu as pltpu
from jax.sharding import PartitionSpec as P

MESH = pl.DeviceIdType.MESH
F32 = jnp.float32
BF16 = jnp.bfloat16

NX, NY, NZ = 4, 4, 8
BLOCKS = 2
LINES, PLANES, BEAMS = (1,2,2,3), (4,4,5,5), (8,8,8,8)
CHUNKS, AHEAD = 4, 4
SIN = (4.442882834149665, -7.308241154529405, 3.6062889579421076, -0.8457635944249917, 0.10920575020378133)
COS = (1.414213496564824, -6.978850988209009, 5.739461169968767, -1.8835629820109427, 0.3106981797730274)
SIN_SHORT = (4.442867902991959, -7.3074434197428175, 3.5947880638880885, -0.7843739922969518)
COS_SHORT = (1.4142040804388327, -6.977642054046934, 5.715238359077324, -1.728348549561637)


def horner(coefs, z):
    total = jnp.full_like(z, coefs[-1])
    for c in coefs[-2::-1]:
        total = total * z + c
    return total


def cos_sin_turns(turns, sin_coefs, cos_coefs):
    r = turns - jnp.round(turns)
    z = r * r
    s = r * horner(sin_coefs, z)
    c = horner(cos_coefs, z)
    return 1.0 - s * s, s * c


def device(y, z, x, core):
    return {"seg": (y // 2) * 2 + core, "mic": (z * NX + x) * 2 + y % 2}


def kernel(
    time_ref, bin_ref, mic_hbm, grid_hbm, out_ref,
    mic_ref, grid_ref, s_sem, tbuf, wt, own, kept, inbox, gathered, steering, acc, right, sent, received, micf, pointf,
    t_sem, p_send, p_recv, z_send, z_recv, m_send, m_recv, l_send, l_recv, b_send, b_recv,
):
    seg = lax.axis_index("seg")
    mic = lax.axis_index("mic")
    core = seg % 2
    y_hi, y_lo = seg // 2, mic % 2
    y = y_hi * 2 + y_lo
    x = (mic // 2) % NX
    z = mic // (2 * NX)
    zp = z // 2
    sibling = device(y, z, x, 1 - core)
    z_peer = [device(y, (z + d) % NZ, x, core) for d in range(NZ)]
    x_peer = [device(y, z, (x + d) % NX, core) for d in range(NX)]
    y_peer = [device((y + d) % NY, z, x, core) for d in range(NY)]

    seg_dev, mic_dev, samples = time_ref.shape
    mic_half = mic_dev // 2
    chunks, per = tbuf.shape[0], tbuf.shape[1]

    def time_copy(i):
        side = (1 - core) if i < chunks // 2 else core
        first = (i % (chunks // 2)) * per
        src = time_ref.at[pl.ds(first, per), pl.ds(side * mic_half, mic_half)]
        return pltpu.make_async_copy(src, tbuf.at[i], t_sem.at[i])

    small = [
        pltpu.make_async_copy(src, dst, s_sem.at[i])
        for i, (src, dst) in enumerate(((mic_hbm, mic_ref), (grid_hbm, grid_ref)))
    ]
    for c in small:
        c.start()
    ahead = AHEAD
    for i in range(ahead):
        time_copy(i).start()

    barrier = pltpu.get_barrier_semaphore()
    peers = [sibling] + z_peer[1:] + x_peer[1:] + y_peer[1:]
    for peer in peers:
        pl.semaphore_signal(barrier, inc=1, device_id=peer, device_id_type=MESH)

    order = bin_ref[0]
    t = lax.broadcasted_iota(jnp.int32, (8, samples), 1)
    turned = (order * t) & (samples - 1)
    inv = 1.0 / samples
    wcos, _ = cos_sin_turns(t.astype(F32) * inv, SIN, COS)
    ca, sa = cos_sin_turns(turned.astype(F32) * inv, SIN, COS)
    window = 0.5 - 0.5 * wcos
    rows = jnp.concatenate([window * ca] * 8 + [-(window * sa)] * 8, axis=0)
    wt[...] = rows.T.astype(BF16)

    lane = lax.broadcasted_iota(jnp.int32, (mic_half, 128), 1) & 63

    def spectra(first_chunk):
        own_sum = jnp.zeros((mic_half, 128), F32)
        for i in range(chunks // 2):
            time_copy(first_chunk + i).wait()
            if first_chunk + i + ahead < chunks:
                time_copy(first_chunk + i + ahead).start()
            part = jnp.dot(
                tbuf[first_chunk + i].reshape(per * mic_half, samples), wt[...], preferred_element_type=F32
            )
            for k in range(per):
                hit = lane == core * seg_dev + i * per + k
                own_sum = jnp.where(hit, part[k * mic_half:(k + 1) * mic_half], own_sum)
        return own_sum.astype(BF16).reshape(2, 16, 128)

    def push(src, dst, send, recv, peer):
        return pltpu.make_async_remote_copy(
            src_ref=src, dst_ref=dst, send_sem=send, recv_sem=recv, device_id=peer, device_id_type=MESH
        )

    own[...] = spectra(0)
    kept[...] = spectra(chunks // 2)
    pair_copy = push(own, inbox, p_send, p_recv, sibling)
    pl.semaphore_wait(barrier, len(peers))
    pair_copy.start()
    acc[...] = jnp.zeros_like(acc)

    def split(v):
        coarse = jnp.floor(v * (1.0 / 64.0) + 0.5) * 64.0
        return coarse, v - coarse

    def split3(v):
        top = jnp.floor(v * (1.0 / 65536.0)) * 65536.0
        rest = v - top
        mid = jnp.floor(rest * (1.0 / 256.0)) * 256.0
        return top, mid, rest - mid

    def rows_of(v, fold):
        hi, lo = split(v)
        sq = v * v
        top, mid, low = split3(sq[0:1] + sq[1:2] + sq[2:3])
        one = jnp.ones_like(top)
        tiny = jnp.full_like(top, 2.0**-20)
        zero = jnp.zeros((13, v.shape[1]), F32)
        if fold:
            return jnp.concatenate([-2.0 * hi, -2.0 * hi, -2.0 * lo, -2.0 * lo, one, one, one, top, mid, low, tiny, zero], axis=0)
        return jnp.concatenate([hi, lo, hi, lo, top, mid, low, one, one, one, tiny, zero], axis=0)

    for c in small:
        c.wait()
    width = out_ref.shape[1]
    pts = grid_ref[:, pl.ds(pl.multiple_of(y_hi * 2 * width, 128), 2 * width)].astype(F32)
    pointf[...] = rows_of(pts, False).T.astype(BF16)
    mine = gathered.at[y_hi, z, x, y_lo]

    def z_copy(d):
        return push(mine, mine, z_send.at[d], z_recv.at[z], z_peer[d])

    pair_copy.wait_recv()
    mine[...] = kept[...] + inbox[...]
    for d in (4, 3, 5, 2, 6, 1, 7):
        z_copy(d).start()

    every = rows_of(mic_ref[...].astype(F32), True).astype(BF16)
    part = 8 * mic_dev
    parts = every.shape[1] // part
    stacked = jnp.concatenate([every[:, i * part:(i + 1) * part] for i in range(parts)], axis=0)
    src = lax.broadcasted_iota(jnp.int32, (part, part // 2), 0)
    dst = lax.broadcasted_iota(jnp.int32, (part, part // 2), 1)
    wanted = (dst // mic_half) * mic_dev + core * mic_half + (dst & (mic_half - 1))
    pick = jnp.where(src == wanted, 1.0, 0.0).astype(BF16)
    picked = jnp.dot(stacked, pick, preferred_element_type=F32).astype(BF16)
    micf[...] = jnp.concatenate([picked[i * 32:(i + 1) * 32] for i in range(parts)], axis=1)
    turns_per_mm = order.astype(F32) * F32(0.001 * 51200.0 / 343.0 / samples)

    groups, depth = steering.shape[0], steering.shape[2] // 2
    blocks = BLOCKS
    tall = 128

    def pair(k):
        return (zp + k * (k + 1) // 2) % groups

    def steer(j):
        g = pair(j // blocks)
        feat = micf[:, pl.ds(pl.multiple_of(g * depth, depth), depth)]
        span = 2 * width // blocks
        for i in range(span // tall):
            rows = pl.ds(pl.multiple_of((j % blocks) * span + i * tall, tall), tall)
            d2 = jnp.dot(pointf[rows, :], feat, preferred_element_type=F32)
            turns = (d2 * turns_per_mm) * lax.rsqrt(d2)
            ca, sa = cos_sin_turns(turns, SIN_SHORT, COS_SHORT)
            steering[g, rows, pl.ds(0, depth)] = ca.astype(BF16)
            steering[g, rows, pl.ds(depth, depth)] = sa.astype(BF16)

    q1, q2 = 0, 1

    def line(k, yy, xx, q):
        return gathered.at[yy // 2, pl.ds(2 * pair(k), 2), xx, yy % 2, q]

    def plane1(k, yy):
        return gathered.at[yy // 2, pl.ds(2 * pair(k), 2), :, yy % 2, q1]

    def plane2(k, xx):
        return gathered.at[:, pl.ds(2 * pair(k), 2), xx, :, q2]

    def z_arrived(k):
        for b in range(2):
            zz = 2 * pair(k) + b

            @pl.when(zz != z)
            def _():
                src = gathered.at[y_hi, zz, x, y_lo]
                push(src, src, z_send.at[1], z_recv.at[zz], z_peer[1]).wait_recv()

    def line_copies(k, d, back):
        xx, yy = ((x + NX - d) % NX, (y + NY - d) % NY) if back else (x, y)
        p1, p2 = line(k, y, xx, q1), line(k, yy, x, q2)
        return (
            push(p1, p1, m_send.at[0, k, d], m_recv.at[0, k, d], x_peer[d]),
            push(p2, p2, m_send.at[1, k, d], m_recv.at[1, k, d], y_peer[d]),
        )

    def plane_copies(k, d, back):
        xx, yy = ((x + NX - d) % NX, (y + NY - d) % NY) if back else (x, y)
        p1, p2 = plane1(k, yy), plane2(k, xx)
        return (
            push(p1, p1, l_send.at[0, k, d], l_recv.at[0, k, d], y_peer[d]),
            push(p2, p2, l_send.at[1, k, d], l_recv.at[1, k, d], x_peer[d]),
        )

    def begin(copies, k):
        for d in (2, 1, 3):
            for c in copies(k, d, False):
                c.start()

    def arrived(copies, k):
        for d in (1, 3, 2):
            for c in copies(k, d, True):
                c.wait_recv()

    def flown(copies, k):
        for d in (1, 3, 2):
            for c in copies(k, d, False):
                c.wait_send()

    piece = width // 2

    def rows_at(side, r):
        return pl.ds(pl.multiple_of(side * width + r * piece, piece), piece)

    def beam_copy(r):
        return push(sent.at[r], received.at[r], b_send.at[r], b_recv.at[r], sibling)

    def turned_spectra(k):
        zs = pl.ds(2 * pair(k), 2)
        sides = [gathered[h, zs].reshape(depth, 128) for h in range(2)]
        sign = jnp.where(lax.broadcasted_iota(jnp.int32, (depth, 128), 1) < 64, -1.0, 1.0)
        turned = [(pltpu.roll(v.astype(F32), 64, 1) * sign).astype(BF16) for v in sides]
        right[...] = jnp.concatenate(
            [jnp.concatenate(sides, axis=1), jnp.concatenate(turned, axis=1)], axis=0
        )

    def beams(k, rows):
        return acc[rows, :] + jnp.dot(steering[pair(k), rows, :], right[...], preferred_element_type=F32)

    steps = groups * blocks

    def at_step(j, when, event):
        first = sum(jnp.where(j > w, 1, 0) for w in when)
        last = sum(jnp.where(j >= w, 1, 0) for w in when)

        def body(k, carry):
            event(k)
            return carry

        lax.fori_loop(first, last, body, 0)

    def lines_event(k):
        z_arrived(k)
        begin(line_copies, k)

    def planes_event(k):
        arrived(line_copies, k)
        begin(plane_copies, k)

    def beams_event(k):
        arrived(plane_copies, k)
        turned_spectra(k)

        def theirs(r, carry):
            rows = rows_at(1 - core, r)
            total = beams(k, rows)

            @pl.when(k < groups - 1)
            def _():
                acc[rows, :] = total

            @pl.when(k == groups - 1)
            def _():
                sent[r] = total
                beam_copy(r).start()

            return carry

        lax.fori_loop(0, 2, theirs, 0)

        def ours(r, carry):
            rows = rows_at(core, r)
            acc[rows, :] = beams(k, rows)
            return carry

        lax.fori_loop(0, 2, ours, 0)

    def step(j, carry):
        pl.when(j < steps)(lambda: steer(j))
        at_step(j, LINES, lines_event)
        at_step(j, PLANES, planes_event)
        at_step(j, BEAMS, beams_event)
        return carry

    lax.fori_loop(0, BEAMS[-1] + 1, step, 0)

    scale = 1.0 / (seg_dev * lax.axis_size("seg") * mic_dev * lax.axis_size("mic") * 0.375 * samples)
    for r in range(2):
        beam_copy(r).wait_recv()
        total = acc[rows_at(core, r), :] + received[r]
        power = total * total
        power = power[:, :128] + power[:, 128:]
        out_ref[:, pl.ds(r * piece, piece)] = jnp.sum(power.T, axis=0, keepdims=True) * scale

    pair_copy.wait_send()
    for r in range(2):
        beam_copy(r).wait_send()
    for d in range(1, NZ):
        z_copy(d).wait_send()

    def drain(k, carry):
        flown(line_copies, k)
        flown(plane_copies, k)
        return carry

    lax.fori_loop(0, groups, drain, 0)


def shards(time_data, order_bin, mic_pos, grid_pos):
    seg_dev, mic_dev, samples = time_data.shape
    width = grid_pos.shape[1] // lax.axis_size("seg")
    mics = mic_pos.shape[1]
    chunks = CHUNKS
    dma = pltpu.SemaphoreType.DMA
    return pl.pallas_call(
        kernel,
        out_shape=jax.ShapeDtypeStruct((1, width), F32),
        in_specs=[
            pl.BlockSpec(memory_space=pltpu.HBM),
            pl.BlockSpec(memory_space=pltpu.SMEM),
            pl.BlockSpec(memory_space=pltpu.HBM),
            pl.BlockSpec(memory_space=pltpu.HBM),
        ],
        out_specs=pl.BlockSpec(memory_space=pltpu.VMEM),
        scratch_shapes=[
            pltpu.VMEM(mic_pos.shape, jnp.int32),
            pltpu.VMEM(grid_pos.shape, jnp.int32),
            pltpu.SemaphoreType.DMA((2,)),
            pltpu.VMEM((chunks, 2 * seg_dev // chunks, mic_dev // 2, samples), BF16),
            pltpu.VMEM((samples, 128), BF16),
            pltpu.VMEM((2, 16, 128), BF16),
            pltpu.VMEM((2, 16, 128), BF16),
            pltpu.VMEM((2, 16, 128), BF16),
            pltpu.VMEM((2, NZ, NX, 2, 2, 16, 128), BF16),
            pltpu.VMEM((4, 2 * width, mics // 4), BF16),
            pltpu.VMEM((2 * width, 256), F32),
            pltpu.VMEM((mics // 4, 256), BF16),
            pltpu.VMEM((2, width // 2, 256), F32),
            pltpu.VMEM((2, width // 2, 256), F32),
            pltpu.VMEM((32, mics // 2), BF16),
            pltpu.VMEM((2 * width, 32), BF16),
            dma((chunks,)),
            dma, dma,
            dma((NZ,)), dma((NZ,)),
            dma((2, 4, NX)), dma((2, 4, NX)),
            dma((2, 4, NX)), dma((2, 4, NX)),
            dma((2,)), dma((2,)),
        ],
        compiler_params=pltpu.CompilerParams(
            collective_id=0, has_side_effects=True, vmem_limit_bytes=55208 << 10
        ),
        name="beamform",
    )(time_data, order_bin, mic_pos, grid_pos)


def solution(mesh):
    placed = (P("seg", "mic", None), P(), P(), P(None, "mic"))
    return jax.shard_map(
        shards, mesh=mesh, in_specs=placed, out_specs=P("mic", "seg"), check_vma=False
    )
```

```python
import functools
import math

import jax
import jax.numpy as jnp
from jax import lax
from jax.experimental import pallas as pl
from jax.experimental.pallas import tpu as pltpu
from jax.sharding import PartitionSpec as P

MESH = pl.DeviceIdType.MESH
F32 = jnp.float32
BF16 = jnp.bfloat16

NX, NY, NZ = 4, 4, 8
BLOCKS = 2
LINES, PLANES, BEAMS = (1,2,2,3), (4,4,5,5), (8,8,8,8)
CHUNKS, AHEAD = 4, 4
SIN = (4.442882834149665, -7.308241154529405, 3.6062889579421076, -0.8457635944249917, 0.10920575020378133)
COS = (1.414213496564824, -6.978850988209009, 5.739461169968767, -1.8835629820109427, 0.3106981797730274)
SIN_SHORT = (4.442867902991959, -7.3074434197428175, 3.5947880638880885, -0.7843739922969518)
COS_SHORT = (1.4142040804388327, -6.977642054046934, 5.715238359077324, -1.728348549561637)


def horner(coefs, z):
    total = jnp.full_like(z, coefs[-1])
    for c in coefs[-2::-1]:
        total = total * z + c
    return total


def cos_sin_turns(turns, sin_coefs, cos_coefs):
    r = turns - jnp.round(turns)
    z = r * r
    s = r * horner(sin_coefs, z)
    c = horner(cos_coefs, z)
    return 1.0 - s * s, s * c


def device(y, z, x, core):
    return {"seg": (y // 2) * 2 + core, "mic": (z * NX + x) * 2 + y % 2}


def kernel(
    time_ref, bin_ref, mic_hbm, grid_hbm, out_ref,
    mic_ref, grid_ref, s_sem, tbuf, wt, own, kept, inbox, gathered, steering, acc, right, sent, received, micf, pointf,
    t_sem, p_send, p_recv, z_send, z_recv, m_send, m_recv, l_send, l_recv, b_send, b_recv,
):
    seg = lax.axis_index("seg")
    mic = lax.axis_index("mic")
    core = seg % 2
    y_hi, y_lo = seg // 2, mic % 2
    y = y_hi * 2 + y_lo
    x = (mic // 2) % NX
    z = mic // (2 * NX)
    zp = z // 2
    sibling = device(y, z, x, 1 - core)
    z_peer = [device(y, (z + d) % NZ, x, core) for d in range(NZ)]
    x_peer = [device(y, z, (x + d) % NX, core) for d in range(NX)]
    y_peer = [device((y + d) % NY, z, x, core) for d in range(NY)]

    barrier = pltpu.get_barrier_semaphore()
    peers = [z_peer[d] for d in (4, 3, 5, 2, 6)] + [x_peer[2], y_peer[2]]
    peers += [z_peer[d] for d in (1, 7)] + [p[d] for p in (x_peer, y_peer) for d in (1, 3)] + [sibling]
    for peer in peers:
        pl.semaphore_signal(barrier, inc=1, device_id=peer, device_id_type=MESH)

    seg_dev, mic_dev, samples = time_ref.shape
    mic_half = mic_dev // 2
    chunks, per = tbuf.shape[0], tbuf.shape[1]

    def time_copy(i):
        side = (1 - core) if i < chunks // 2 else core
        first = (i % (chunks // 2)) * per
        src = time_ref.at[pl.ds(first, per), pl.ds(side * mic_half, mic_half)]
        return pltpu.make_async_copy(src, tbuf.at[i], t_sem.at[i])

    small = [
        pltpu.make_async_copy(src, dst, s_sem.at[i])
        for i, (src, dst) in enumerate(((mic_hbm, mic_ref), (grid_hbm, grid_ref)))
    ]
    for c in small:
        c.start()
    ahead = AHEAD
    for i in range(ahead):
        time_copy(i).start()

    order = bin_ref[0]
    t = lax.broadcasted_iota(jnp.int32, (8, samples), 1)
    turned = (order * t) & (samples - 1)
    inv = 1.0 / samples
    wcos, _ = cos_sin_turns(t.astype(F32) * inv, SIN, COS)
    ca, sa = cos_sin_turns(turned.astype(F32) * inv, SIN, COS)
    window = 0.5 - 0.5 * wcos
    rows = jnp.concatenate([window * ca] * 8 + [-(window * sa)] * 8, axis=0)
    wt[...] = rows.T.astype(BF16)

    lane = lax.broadcasted_iota(jnp.int32, (mic_half, 128), 1) & 63

    def spectra(first_chunk):
        own_sum = jnp.zeros((mic_half, 128), F32)
        for i in range(chunks // 2):
            time_copy(first_chunk + i).wait()
            if first_chunk + i + ahead < chunks:
                time_copy(first_chunk + i + ahead).start()
            part = jnp.dot(
                tbuf[first_chunk + i].reshape(per * mic_half, samples), wt[...], preferred_element_type=F32
            )
            for k in range(per):
                hit = lane == core * seg_dev + i * per + k
                own_sum = jnp.where(hit, part[k * mic_half:(k + 1) * mic_half], own_sum)
        return own_sum.astype(BF16).reshape(2, 16, 128)

    def push(src, dst, send, recv, peer):
        return pltpu.make_async_remote_copy(
            src_ref=src, dst_ref=dst, send_sem=send, recv_sem=recv, device_id=peer, device_id_type=MESH
        )

    own[...] = spectra(0)
    kept[...] = spectra(chunks // 2)
    pair_copy = push(own, inbox, p_send, p_recv, sibling)
    pl.semaphore_wait(barrier, len(peers))
    pair_copy.start()
    acc[...] = jnp.zeros_like(acc)

    def split(v):
        coarse = jnp.floor(v * (1.0 / 64.0) + 0.5) * 64.0
        return coarse, v - coarse

    def split3(v):
        top = jnp.floor(v * (1.0 / 65536.0)) * 65536.0
        rest = v - top
        mid = jnp.floor(rest * (1.0 / 256.0)) * 256.0
        return top, mid, rest - mid

    def rows_of(v, fold):
        hi, lo = split(v)
        sq = v * v
        top, mid, low = split3(sq[0:1] + sq[1:2] + sq[2:3])
        one = jnp.ones_like(top)
        tiny = jnp.full_like(top, 2.0**-20)
        zero = jnp.zeros((13, v.shape[1]), F32)
        if fold:
            return jnp.concatenate([-2.0 * hi, -2.0 * hi, -2.0 * lo, -2.0 * lo, one, one, one, top, mid, low, tiny, zero], axis=0)
        return jnp.concatenate([hi, lo, hi, lo, top, mid, low, one, one, one, tiny, zero], axis=0)

    for c in small:
        c.wait()
    width = out_ref.shape[1]
    pts = grid_ref[:, pl.ds(pl.multiple_of(y_hi * 2 * width, 128), 2 * width)].astype(F32)
    pointf[...] = rows_of(pts, False).T.astype(BF16)
    mine = gathered.at[y_hi, z, x, y_lo]

    def z_copy(d):
        return push(mine, mine, z_send.at[d], z_recv.at[z], z_peer[d])

    pair_copy.wait_recv()
    mine[...] = kept[...] + inbox[...]
    for d in (4, 3, 5, 2, 6, 1, 7):
        z_copy(d).start()

    every = rows_of(mic_ref[...].astype(F32), True).astype(BF16)
    part = 8 * mic_dev
    parts = every.shape[1] // part
    stacked = jnp.concatenate([every[:, i * part:(i + 1) * part] for i in range(parts)], axis=0)
    src = lax.broadcasted_iota(jnp.int32, (part, part // 2), 0)
    dst = lax.broadcasted_iota(jnp.int32, (part, part // 2), 1)
    wanted = (dst // mic_half) * mic_dev + core * mic_half + (dst & (mic_half - 1))
    pick = jnp.where(src == wanted, 1.0, 0.0).astype(BF16)
    picked = jnp.dot(stacked, pick, preferred_element_type=F32).astype(BF16)
    micf[...] = jnp.concatenate([picked[i * 32:(i + 1) * 32] for i in range(parts)], axis=1)
    turns_per_mm = order.astype(F32) * F32(0.001 * 51200.0 / 343.0 / samples)

    groups, depth = steering.shape[0], steering.shape[2] // 2
    blocks = BLOCKS
    tall = 128

    def pair(k):
        return (zp + k * (k + 1) // 2) % groups

    def steer(j):
        g = pair(j // blocks)
        feat = micf[:, pl.ds(pl.multiple_of(g * depth, depth), depth)]
        span = 2 * width // blocks
        for i in range(span // tall):
            rows = pl.ds(pl.multiple_of((j % blocks) * span + i * tall, tall), tall)
            d2 = jnp.dot(pointf[rows, :], feat, preferred_element_type=F32)
            turns = (d2 * turns_per_mm) * lax.rsqrt(d2)
            ca, sa = cos_sin_turns(turns, SIN_SHORT, COS_SHORT)
            steering[g, rows, pl.ds(0, depth)] = ca.astype(BF16)
            steering[g, rows, pl.ds(depth, depth)] = sa.astype(BF16)

    q1, q2 = 0, 1

    def line(k, yy, xx, q):
        return gathered.at[yy // 2, pl.ds(2 * pair(k), 2), xx, yy % 2, q]

    def plane1(k, yy):
        return gathered.at[yy // 2, pl.ds(2 * pair(k), 2), :, yy % 2, q1]

    def plane2(k, xx):
        return gathered.at[:, pl.ds(2 * pair(k), 2), xx, :, q2]

    def z_arrived(k):
        for b in range(2):
            zz = 2 * pair(k) + b

            @pl.when(zz != z)
            def _():
                src = gathered.at[y_hi, zz, x, y_lo]
                push(src, src, z_send.at[1], z_recv.at[zz], z_peer[1]).wait_recv()

    def line_copies(k, d, back):
        xx, yy = ((x + NX - d) % NX, (y + NY - d) % NY) if back else (x, y)
        p1, p2 = line(k, y, xx, q1), line(k, yy, x, q2)
        return (
            push(p1, p1, m_send.at[0, k, d], m_recv.at[0, k, d], x_peer[d]),
            push(p2, p2, m_send.at[1, k, d], m_recv.at[1, k, d], y_peer[d]),
        )

    def plane_copies(k, d, back):
        xx, yy = ((x + NX - d) % NX, (y + NY - d) % NY) if back else (x, y)
        p1, p2 = plane1(k, yy), plane2(k, xx)
        return (
            push(p1, p1, l_send.at[0, k, d], l_recv.at[0, k, d], y_peer[d]),
            push(p2, p2, l_send.at[1, k, d], l_recv.at[1, k, d], x_peer[d]),
        )

    def begin(copies, k):
        for d in (2, 1, 3):
            for c in copies(k, d, False):
                c.start()

    def arrived(copies, k):
        for d in (1, 3, 2):
            for c in copies(k, d, True):
                c.wait_recv()

    def flown(copies, k):
        for d in (1, 3, 2):
            for c in copies(k, d, False):
                c.wait_send()

    piece = width // 2

    def rows_at(side, r):
        return pl.ds(pl.multiple_of(side * width + r * piece, piece), piece)

    def beam_copy(r):
        return push(sent.at[r], received.at[r], b_send.at[r], b_recv.at[r], sibling)

    def turned_spectra(k):
        zs = pl.ds(2 * pair(k), 2)
        sides = [gathered[h, zs].reshape(depth, 128) for h in range(2)]
        sign = jnp.where(lax.broadcasted_iota(jnp.int32, (depth, 128), 1) < 64, -1.0, 1.0)
        turned = [(pltpu.roll(v.astype(F32), 64, 1) * sign).astype(BF16) for v in sides]
        right[...] = jnp.concatenate(
            [jnp.concatenate(sides, axis=1), jnp.concatenate(turned, axis=1)], axis=0
        )

    def beams(k, rows):
        return acc[rows, :] + jnp.dot(steering[pair(k), rows, :], right[...], preferred_element_type=F32)

    steps = groups * blocks

    def at_step(j, when, event):
        first = sum(jnp.where(j > w, 1, 0) for w in when)
        last = sum(jnp.where(j >= w, 1, 0) for w in when)

        def body(k, carry):
            event(k)
            return carry

        lax.fori_loop(first, last, body, 0)

    def lines_event(k):
        z_arrived(k)
        begin(line_copies, k)

    def planes_event(k):
        arrived(line_copies, k)
        begin(plane_copies, k)

    def beams_event(k):
        arrived(plane_copies, k)
        turned_spectra(k)

        def theirs(r, carry):
            rows = rows_at(1 - core, r)
            total = beams(k, rows)

            @pl.when(k < groups - 1)
            def _():
                acc[rows, :] = total

            @pl.when(k == groups - 1)
            def _():
                sent[r] = total
                beam_copy(r).start()

            return carry

        lax.fori_loop(0, 2, theirs, 0)

        def ours(r, carry):
            rows = rows_at(core, r)
            acc[rows, :] = beams(k, rows)
            return carry

        lax.fori_loop(0, 2, ours, 0)

    def step(j, carry):
        pl.when(j < steps)(lambda: steer(j))
        at_step(j, LINES, lines_event)
        at_step(j, PLANES, planes_event)
        at_step(j, BEAMS, beams_event)
        return carry

    lax.fori_loop(0, BEAMS[-1] + 1, step, 0)

    scale = 1.0 / (seg_dev * lax.axis_size("seg") * mic_dev * lax.axis_size("mic") * 0.375 * samples)
    for r in range(2):
        beam_copy(r).wait_recv()
        total = acc[rows_at(core, r), :] + received[r]
        power = total * total
        power = power[:, :128] + power[:, 128:]
        out_ref[:, pl.ds(r * piece, piece)] = jnp.sum(power.T, axis=0, keepdims=True) * scale

    pair_copy.wait_send()
    for r in range(2):
        beam_copy(r).wait_send()
    for d in range(1, NZ):
        z_copy(d).wait_send()

    def drain(k, carry):
        flown(line_copies, k)
        flown(plane_copies, k)
        return carry

    lax.fori_loop(0, groups, drain, 0)


def shards(time_data, order_bin, mic_pos, grid_pos):
    seg_dev, mic_dev, samples = time_data.shape
    width = grid_pos.shape[1] // lax.axis_size("seg")
    mics = mic_pos.shape[1]
    chunks = CHUNKS
    dma = pltpu.SemaphoreType.DMA
    return pl.pallas_call(
        kernel,
        out_shape=jax.ShapeDtypeStruct((1, width), F32),
        in_specs=[
            pl.BlockSpec(memory_space=pltpu.HBM),
            pl.BlockSpec(memory_space=pltpu.SMEM),
            pl.BlockSpec(memory_space=pltpu.HBM),
            pl.BlockSpec(memory_space=pltpu.HBM),
        ],
        out_specs=pl.BlockSpec(memory_space=pltpu.VMEM),
        scratch_shapes=[
            pltpu.VMEM(mic_pos.shape, jnp.int32),
            pltpu.VMEM(grid_pos.shape, jnp.int32),
            pltpu.SemaphoreType.DMA((2,)),
            pltpu.VMEM((chunks, 2 * seg_dev // chunks, mic_dev // 2, samples), BF16),
            pltpu.VMEM((samples, 128), BF16),
            pltpu.VMEM((2, 16, 128), BF16),
            pltpu.VMEM((2, 16, 128), BF16),
            pltpu.VMEM((2, 16, 128), BF16),
            pltpu.VMEM((2, NZ, NX, 2, 2, 16, 128), BF16),
            pltpu.VMEM((4, 2 * width, mics // 4), BF16),
            pltpu.VMEM((2 * width, 256), F32),
            pltpu.VMEM((mics // 4, 256), BF16),
            pltpu.VMEM((2, width // 2, 256), F32),
            pltpu.VMEM((2, width // 2, 256), F32),
            pltpu.VMEM((32, mics // 2), BF16),
            pltpu.VMEM((2 * width, 32), BF16),
            dma((chunks,)),
            dma, dma,
            dma((NZ,)), dma((NZ,)),
            dma((2, 4, NX)), dma((2, 4, NX)),
            dma((2, 4, NX)), dma((2, 4, NX)),
            dma((2,)), dma((2,)),
        ],
        compiler_params=pltpu.CompilerParams(
            collective_id=0, has_side_effects=True, vmem_limit_bytes=55208 << 10
        ),
        name="beamform",
    )(time_data, order_bin, mic_pos, grid_pos)


def solution(mesh):
    placed = (P("seg", "mic", None), P(), P(), P(None, "mic"))
    return jax.shard_map(
        shards, mesh=mesh, in_specs=placed, out_specs=P("mic", "seg"), check_vma=False
    )
```

```python
import functools
import math

import jax
import jax.numpy as jnp
from jax import lax
from jax.experimental import pallas as pl
from jax.experimental.pallas import tpu as pltpu
from jax.sharding import PartitionSpec as P

MESH = pl.DeviceIdType.MESH
F32 = jnp.float32
BF16 = jnp.bfloat16

NX, NY, NZ = 4, 4, 8
BLOCKS = 2
LINES, PLANES, BEAMS = (1,2,2,3), (4,4,5,5), (8,8,8,8)
CHUNKS, AHEAD = 8, 8
SIN = (4.442882834149665, -7.308241154529405, 3.6062889579421076, -0.8457635944249917, 0.10920575020378133)
COS = (1.414213496564824, -6.978850988209009, 5.739461169968767, -1.8835629820109427, 0.3106981797730274)
SIN_SHORT = (4.442867902991959, -7.3074434197428175, 3.5947880638880885, -0.7843739922969518)
COS_SHORT = (1.4142040804388327, -6.977642054046934, 5.715238359077324, -1.728348549561637)


def horner(coefs, z):
    total = jnp.full_like(z, coefs[-1])
    for c in coefs[-2::-1]:
        total = total * z + c
    return total


def cos_sin_turns(turns, sin_coefs, cos_coefs):
    r = turns - jnp.round(turns)
    z = r * r
    s = r * horner(sin_coefs, z)
    c = horner(cos_coefs, z)
    return 1.0 - s * s, s * c


def device(y, z, x, core):
    return {"seg": (y // 2) * 2 + core, "mic": (z * NX + x) * 2 + y % 2}


def kernel(
    time_ref, bin_ref, mic_hbm, grid_hbm, out_ref,
    mic_ref, grid_ref, s_sem, tbuf, wt, own, kept, inbox, gathered, steering, acc, right, sent, received, micf, pointf,
    t_sem, p_send, p_recv, z_send, z_recv, m_send, m_recv, l_send, l_recv, b_send, b_recv,
):
    seg = lax.axis_index("seg")
    mic = lax.axis_index("mic")
    core = seg % 2
    y_hi, y_lo = seg // 2, mic % 2
    y = y_hi * 2 + y_lo
    x = (mic // 2) % NX
    z = mic // (2 * NX)
    zp = z // 2
    sibling = device(y, z, x, 1 - core)
    z_peer = [device(y, (z + d) % NZ, x, core) for d in range(NZ)]
    x_peer = [device(y, z, (x + d) % NX, core) for d in range(NX)]
    y_peer = [device((y + d) % NY, z, x, core) for d in range(NY)]

    seg_dev, mic_dev, samples = time_ref.shape
    mic_half = mic_dev // 2
    chunks, per = tbuf.shape[0], tbuf.shape[1]

    def time_copy(i):
        side = (1 - core) if i < chunks // 2 else core
        first = (i % (chunks // 2)) * per
        src = time_ref.at[pl.ds(first, per), pl.ds(side * mic_half, mic_half)]
        return pltpu.make_async_copy(src, tbuf.at[i], t_sem.at[i])

    small = [
        pltpu.make_async_copy(src, dst, s_sem.at[i])
        for i, (src, dst) in enumerate(((mic_hbm, mic_ref), (grid_hbm, grid_ref)))
    ]
    for c in small:
        c.start()
    ahead = AHEAD
    for i in range(ahead):
        time_copy(i).start()

    barrier = pltpu.get_barrier_semaphore()
    peers = [sibling] + z_peer[1:] + x_peer[1:] + y_peer[1:]
    for peer in peers:
        pl.semaphore_signal(barrier, inc=1, device_id=peer, device_id_type=MESH)

    order = bin_ref[0]
    t = lax.broadcasted_iota(jnp.int32, (8, samples), 1)
    turned = (order * t) & (samples - 1)
    inv = 1.0 / samples
    wcos, _ = cos_sin_turns(t.astype(F32) * inv, SIN, COS)
    ca, sa = cos_sin_turns(turned.astype(F32) * inv, SIN, COS)
    window = 0.5 - 0.5 * wcos
    rows = jnp.concatenate([window * ca] * 8 + [-(window * sa)] * 8, axis=0)
    wt[...] = rows.T.astype(BF16)

    lane = lax.broadcasted_iota(jnp.int32, (mic_half, 128), 1) & 63

    def spectra(first_chunk):
        own_sum = jnp.zeros((mic_half, 128), F32)
        for i in range(chunks // 2):
            time_copy(first_chunk + i).wait()
            if first_chunk + i + ahead < chunks:
                time_copy(first_chunk + i + ahead).start()
            part = jnp.dot(
                tbuf[first_chunk + i].reshape(per * mic_half, samples), wt[...], preferred_element_type=F32
            )
            for k in range(per):
                hit = lane == core * seg_dev + i * per + k
                own_sum = jnp.where(hit, part[k * mic_half:(k + 1) * mic_half], own_sum)
        return own_sum.astype(BF16).reshape(2, 16, 128)

    def push(src, dst, send, recv, peer):
        return pltpu.make_async_remote_copy(
            src_ref=src, dst_ref=dst, send_sem=send, recv_sem=recv, device_id=peer, device_id_type=MESH
        )

    own[...] = spectra(0)
    kept[...] = spectra(chunks // 2)
    pair_copy = push(own, inbox, p_send, p_recv, sibling)
    pl.semaphore_wait(barrier, len(peers))
    pair_copy.start()
    acc[...] = jnp.zeros_like(acc)

    def split(v):
        coarse = jnp.floor(v * (1.0 / 64.0) + 0.5) * 64.0
        return coarse, v - coarse

    def split3(v):
        top = jnp.floor(v * (1.0 / 65536.0)) * 65536.0
        rest = v - top
        mid = jnp.floor(rest * (1.0 / 256.0)) * 256.0
        return top, mid, rest - mid

    def rows_of(v, fold):
        hi, lo = split(v)
        sq = v * v
        top, mid, low = split3(sq[0:1] + sq[1:2] + sq[2:3])
        one = jnp.ones_like(top)
        tiny = jnp.full_like(top, 2.0**-20)
        zero = jnp.zeros((13, v.shape[1]), F32)
        if fold:
            return jnp.concatenate([-2.0 * hi, -2.0 * hi, -2.0 * lo, -2.0 * lo, one, one, one, top, mid, low, tiny, zero], axis=0)
        return jnp.concatenate([hi, lo, hi, lo, top, mid, low, one, one, one, tiny, zero], axis=0)

    for c in small:
        c.wait()
    width = out_ref.shape[1]
    pts = grid_ref[:, pl.ds(pl.multiple_of(y_hi * 2 * width, 128), 2 * width)].astype(F32)
    pointf[...] = rows_of(pts, False).T.astype(BF16)
    mine = gathered.at[y_hi, z, x, y_lo]

    def z_copy(d):
        return push(mine, mine, z_send.at[d], z_recv.at[z], z_peer[d])

    pair_copy.wait_recv()
    mine[...] = kept[...] + inbox[...]
    for d in (4, 3, 5, 2, 6, 1, 7):
        z_copy(d).start()

    every = rows_of(mic_ref[...].astype(F32), True).astype(BF16)
    part = 8 * mic_dev
    parts = every.shape[1] // part
    stacked = jnp.concatenate([every[:, i * part:(i + 1) * part] for i in range(parts)], axis=0)
    src = lax.broadcasted_iota(jnp.int32, (part, part // 2), 0)
    dst = lax.broadcasted_iota(jnp.int32, (part, part // 2), 1)
    wanted = (dst // mic_half) * mic_dev + core * mic_half + (dst & (mic_half - 1))
    pick = jnp.where(src == wanted, 1.0, 0.0).astype(BF16)
    picked = jnp.dot(stacked, pick, preferred_element_type=F32).astype(BF16)
    micf[...] = jnp.concatenate([picked[i * 32:(i + 1) * 32] for i in range(parts)], axis=1)
    turns_per_mm = order.astype(F32) * F32(0.001 * 51200.0 / 343.0 / samples)

    groups, depth = steering.shape[0], steering.shape[2] // 2
    blocks = BLOCKS
    tall = 128

    def pair(k):
        return (zp + k * (k + 1) // 2) % groups

    def steer(j):
        g = pair(j // blocks)
        feat = micf[:, pl.ds(pl.multiple_of(g * depth, depth), depth)]
        span = 2 * width // blocks
        for i in range(span // tall):
            rows = pl.ds(pl.multiple_of((j % blocks) * span + i * tall, tall), tall)
            d2 = jnp.dot(pointf[rows, :], feat, preferred_element_type=F32)
            turns = (d2 * turns_per_mm) * lax.rsqrt(d2)
            ca, sa = cos_sin_turns(turns, SIN_SHORT, COS_SHORT)
            steering[g, rows, pl.ds(0, depth)] = ca.astype(BF16)
            steering[g, rows, pl.ds(depth, depth)] = sa.astype(BF16)

    q1, q2 = 0, 1

    def line(k, yy, xx, q):
        return gathered.at[yy // 2, pl.ds(2 * pair(k), 2), xx, yy % 2, q]

    def plane1(k, yy):
        return gathered.at[yy // 2, pl.ds(2 * pair(k), 2), :, yy % 2, q1]

    def plane2(k, xx):
        return gathered.at[:, pl.ds(2 * pair(k), 2), xx, :, q2]

    def z_arrived(k):
        for b in range(2):
            zz = 2 * pair(k) + b

            @pl.when(zz != z)
            def _():
                src = gathered.at[y_hi, zz, x, y_lo]
                push(src, src, z_send.at[1], z_recv.at[zz], z_peer[1]).wait_recv()

    def line_copies(k, d, back):
        xx, yy = ((x + NX - d) % NX, (y + NY - d) % NY) if back else (x, y)
        p1, p2 = line(k, y, xx, q1), line(k, yy, x, q2)
        return (
            push(p1, p1, m_send.at[0, k, d], m_recv.at[0, k, d], x_peer[d]),
            push(p2, p2, m_send.at[1, k, d], m_recv.at[1, k, d], y_peer[d]),
        )

    def plane_copies(k, d, back):
        xx, yy = ((x + NX - d) % NX, (y + NY - d) % NY) if back else (x, y)
        p1, p2 = plane1(k, yy), plane2(k, xx)
        return (
            push(p1, p1, l_send.at[0, k, d], l_recv.at[0, k, d], y_peer[d]),
            push(p2, p2, l_send.at[1, k, d], l_recv.at[1, k, d], x_peer[d]),
        )

    def begin(copies, k):
        for d in (2, 1, 3):
            for c in copies(k, d, False):
                c.start()

    def arrived(copies, k):
        for d in (1, 3, 2):
            for c in copies(k, d, True):
                c.wait_recv()

    def flown(copies, k):
        for d in (1, 3, 2):
            for c in copies(k, d, False):
                c.wait_send()

    piece = width // 2

    def rows_at(side, r):
        return pl.ds(pl.multiple_of(side * width + r * piece, piece), piece)

    def beam_copy(r):
        return push(sent.at[r], received.at[r], b_send.at[r], b_recv.at[r], sibling)

    def turned_spectra(k):
        zs = pl.ds(2 * pair(k), 2)
        sides = [gathered[h, zs].reshape(depth, 128) for h in range(2)]
        sign = jnp.where(lax.broadcasted_iota(jnp.int32, (depth, 128), 1) < 64, -1.0, 1.0)
        turned = [(pltpu.roll(v.astype(F32), 64, 1) * sign).astype(BF16) for v in sides]
        right[...] = jnp.concatenate(
            [jnp.concatenate(sides, axis=1), jnp.concatenate(turned, axis=1)], axis=0
        )

    def beams(k, rows):
        return acc[rows, :] + jnp.dot(steering[pair(k), rows, :], right[...], preferred_element_type=F32)

    steps = groups * blocks

    def at_step(j, when, event):
        first = sum(jnp.where(j > w, 1, 0) for w in when)
        last = sum(jnp.where(j >= w, 1, 0) for w in when)

        def body(k, carry):
            event(k)
            return carry

        lax.fori_loop(first, last, body, 0)

    def lines_event(k):
        z_arrived(k)
        begin(line_copies, k)

    def planes_event(k):
        arrived(line_copies, k)
        begin(plane_copies, k)

    def beams_event(k):
        arrived(plane_copies, k)
        turned_spectra(k)

        def theirs(r, carry):
            rows = rows_at(1 - core, r)
            total = beams(k, rows)

            @pl.when(k < groups - 1)
            def _():
                acc[rows, :] = total

            @pl.when(k == groups - 1)
            def _():
                sent[r] = total
                beam_copy(r).start()

            return carry

        lax.fori_loop(0, 2, theirs, 0)

        def ours(r, carry):
            rows = rows_at(core, r)
            acc[rows, :] = beams(k, rows)
            return carry

        lax.fori_loop(0, 2, ours, 0)

    def step(j, carry):
        pl.when(j < steps)(lambda: steer(j))
        at_step(j, LINES, lines_event)
        at_step(j, PLANES, planes_event)
        at_step(j, BEAMS, beams_event)
        return carry

    lax.fori_loop(0, BEAMS[-1] + 1, step, 0)

    scale = 1.0 / (seg_dev * lax.axis_size("seg") * mic_dev * lax.axis_size("mic") * 0.375 * samples)
    for r in range(2):
        beam_copy(r).wait_recv()
        total = acc[rows_at(core, r), :] + received[r]
        power = total * total
        power = power[:, :128] + power[:, 128:]
        out_ref[:, pl.ds(r * piece, piece)] = jnp.sum(power.T, axis=0, keepdims=True) * scale

    pair_copy.wait_send()
    for r in range(2):
        beam_copy(r).wait_send()
    for d in range(1, NZ):
        z_copy(d).wait_send()

    def drain(k, carry):
        flown(line_copies, k)
        flown(plane_copies, k)
        return carry

    lax.fori_loop(0, groups, drain, 0)


def shards(time_data, order_bin, mic_pos, grid_pos):
    seg_dev, mic_dev, samples = time_data.shape
    width = grid_pos.shape[1] // lax.axis_size("seg")
    mics = mic_pos.shape[1]
    chunks = CHUNKS
    dma = pltpu.SemaphoreType.DMA
    return pl.pallas_call(
        kernel,
        out_shape=jax.ShapeDtypeStruct((1, width), F32),
        in_specs=[
            pl.BlockSpec(memory_space=pltpu.HBM),
            pl.BlockSpec(memory_space=pltpu.SMEM),
            pl.BlockSpec(memory_space=pltpu.HBM),
            pl.BlockSpec(memory_space=pltpu.HBM),
        ],
        out_specs=pl.BlockSpec(memory_space=pltpu.VMEM),
        scratch_shapes=[
            pltpu.VMEM(mic_pos.shape, jnp.int32),
            pltpu.VMEM(grid_pos.shape, jnp.int32),
            pltpu.SemaphoreType.DMA((2,)),
            pltpu.VMEM((chunks, 2 * seg_dev // chunks, mic_dev // 2, samples), BF16),
            pltpu.VMEM((samples, 128), BF16),
            pltpu.VMEM((2, 16, 128), BF16),
            pltpu.VMEM((2, 16, 128), BF16),
            pltpu.VMEM((2, 16, 128), BF16),
            pltpu.VMEM((2, NZ, NX, 2, 2, 16, 128), BF16),
            pltpu.VMEM((4, 2 * width, mics // 4), BF16),
            pltpu.VMEM((2 * width, 256), F32),
            pltpu.VMEM((mics // 4, 256), BF16),
            pltpu.VMEM((2, width // 2, 256), F32),
            pltpu.VMEM((2, width // 2, 256), F32),
            pltpu.VMEM((32, mics // 2), BF16),
            pltpu.VMEM((2 * width, 32), BF16),
            dma((chunks,)),
            dma, dma,
            dma((NZ,)), dma((NZ,)),
            dma((2, 4, NX)), dma((2, 4, NX)),
            dma((2, 4, NX)), dma((2, 4, NX)),
            dma((2,)), dma((2,)),
        ],
        compiler_params=pltpu.CompilerParams(
            collective_id=0, has_side_effects=True, vmem_limit_bytes=55208 << 10
        ),
        name="beamform",
    )(time_data, order_bin, mic_pos, grid_pos)


def solution(mesh):
    placed = (P("seg", "mic", None), P(), P(), P(None, "mic"))
    return jax.shard_map(
        shards, mesh=mesh, in_specs=placed, out_specs=P("mic", "seg"), check_vma=False
    )
```
